32 devices in a mesh: dp: 8 (over z, core), tensor: 4 (over y, x).
Axes of the slice: x: 2, y: 2, z: 4, core: 2. Of those that a mesh axis runs over, the one named last changes fastest.
Arguments:
- inputs: bfloat16 [12288, 2048], P(('dp', 'tensor')), may hold values from -6 to 6
- cotangent: bfloat16 [12288, 2048], P(('dp', 'tensor')), may hold values from -6 to 6
- routes: int32 [12288, 4], P('dp'), may hold values from 0 to 15, all different within a row; in each aligned block of 1536 rows (0 to 1535, 1536 to 3071, ...) at most 408 rows name the same one
- gain_attn: float32 [2048], replicated, may hold values from 0.5 to 1.5
- w_qkv: float32 [2048, 3, 2048], P('dp', None, 'tensor'), may hold values from -0.125 to 0.125
- qkv_bias: float32 [3, 16, 128], P(None, 'tensor', 'dp'), may hold values from -0.6 to 0.6
- w_out: float32 [2048, 2048], P('dp', 'tensor'), may hold values from -1 to 1
- gain_ffn: float32 [2048], replicated, may hold values from 0.5 to 1.5
- router: float32 [16, 2048], replicated, may hold values from -0.0625 to 0.0625
- shared_gate: float32 [2048], replicated, may hold values from -0.125 to 0.125
- expert_gate_up: float32 [16, 2, 1408, 2048], P(None, None, 'tensor', 'dp'), may hold values from -0.125 to 0.125
- expert_down: float32 [16, 1408, 2048], P(None, 'tensor', 'dp'), may hold values from -2.5 to 2.5
- shared_gate_up: float32 [2048, 2, 5632], P('dp', None, 'tensor'), may hold values from -0.125 to 0.125
- shared_down: float32 [2048, 5632], P('dp', 'tensor'), may hold values from -0.15625 to 0.15625
Outputs:
- layer_out: bfloat16 [12288, 2048], P(('dp', 'tensor'))
- input_grad: float32 [12288, 2048], P(('dp', 'tensor'))
- gain_attn_grad: float32 [2048], P(('dp', 'tensor'))
- w_qkv_grad: float32 [2048, 3, 2048], P('dp', None, 'tensor')
- qkv_bias_grad: float32 [3, 16, 128], P(None, 'tensor', 'dp')
- w_out_grad: float32 [2048, 2048], P('dp', 'tensor')
- gain_ffn_grad: float32 [2048], P(('dp', 'tensor'))
- router_grad: float32 [16, 2048], P(None, ('dp', 'tensor'))
- shared_gate_grad: float32 [2048], P(('dp', 'tensor'))
- expert_gate_up_grad: float32 [16, 2, 1408, 2048], P(None, None, 'tensor', 'dp')
- expert_down_grad: float32 [16, 1408, 2048], P(None, 'tensor', 'dp')
- shared_gate_up_grad: float32 [2048, 2, 5632], P('dp', None, 'tensor')
- shared_down_grad: float32 [2048, 5632], P('dp', 'tensor')
The draws below stay inside these ranges and needn't reach their ends.
Inputs may be any that keep to these rules, and one draw needn't show every extreme that they name: `routes`: in each block of 1536 rows held by one index of dp, every row names 4 different experts, no expert is named by more than 408 rows, a bound that some block reaches.
All inputs are finite; a program needn't handle non-finite values.
Results may differ from the reference program's by a relative error of at most 0.023.
Values may be sent and summed in bfloat16 or wider, within the bound.
No kernel may reach another device: no remote copies, remote signals or barrier semaphores. Data moves between devices by JAX's collectives and lax.ppermute only.
A program may use at most 384 MiB of HBM per device.

```python
import math
import jax
import jax.numpy as jnp
import numpy as np
from jax import lax

D = 2048
HEADS = 16
HEAD_DIM = 128
MOE_FF = 1408
SHARED_FF = 5632
TOP = 4
EXPERTS = 16
PROMPT = 2048
CONT = 256
CONTS = 4
QBLOCK = 512
HID = 2048
BLOCK = 1536
TOKENS = 12288
CAP = 408
N_DP = 8


def level_of(stream_key, dims, cuts, least, largest):
    level = 1.0
    for axis_at, shards_of in cuts:
        draws = jax.random.uniform(jax.random.fold_in(jax.random.fold_in(stream_key, 6), axis_at), (shards_of,), jnp.float32, least / len(cuts), largest / len(cuts))
        level = level * jnp.repeat(jnp.exp(draws), dims[axis_at] // shards_of).reshape((-1,) + (1,) * (len(dims) - 1 - axis_at))
    return level


def deal_out(stream_key, own, number, rows, amount, top, reach, skew):
    sequence = jax.random.permutation(stream_key, amount)
    crowded, usual = load_shares(amount, rows * top, reach, skew, True), load_shares(amount, rows * top, reach, skew, False)
    places = jnp.arange(amount)

    def named(tallies, rotation):
        used = int((tallies > 0).sum())
        fixed = max(1, used // 4)
        shifted = fixed + (places - fixed + rotation * (used - fixed)) % max(1, amount - fixed)
        return jnp.zeros((amount,), jnp.int32).at[sequence[jnp.where(places < fixed, places, shifted)]].set(jnp.asarray(tallies, jnp.int32))

    tallies = jnp.where(number % 4 == 0, named(crowded, number // 4), named(usual, number - number // 4 - 1))
    mixed = jax.random.permutation(jax.random.fold_in(own, 3), amount)
    giver, sink = mixed[0:amount // 2 * 2:2], mixed[1:amount // 2 * 2:2]
    slack = jnp.minimum(tallies[giver] - 1, reach - tallies[sink]) // 2
    slack = jnp.where((giver == sequence[0]) | (sink == sequence[0]) | (tallies[sink] == 0), 0, jnp.maximum(slack, 0))
    shifted = jax.random.randint(jax.random.fold_in(own, 4), (amount // 2,), 0, 1 << 20) % (slack + 1)
    tallies = tallies.at[giver].add(-shifted).at[sink].add(shifted)
    items = jnp.searchsorted(jnp.cumsum(tallies), jnp.arange(rows * top), side="right").astype(jnp.int32)
    grid = items.reshape(top, rows).T
    grid = grid[jax.random.permutation(jax.random.fold_in(own, 1), rows)]
    rotation = jax.random.randint(jax.random.fold_in(own, 2), (rows, 1), 0, top)
    return jnp.take_along_axis(grid, (jnp.arange(top)[None, :] + rotation) % top, axis=1)


def load_shares(number_of, total, limit, skew, full):
    portions = [(1 << 20) // math.isqrt(grade ** skew) + 1 for grade in range(1, number_of + 1)]
    largest = limit if full else min(limit, max(-(-total // number_of), total * portions[0] // sum(portions)))
    least = 1 if total - largest >= number_of - 1 else 0
    holding, spare = [largest] + [least] * (number_of - 1), total - largest - least * (number_of - 1)
    while spare > 0:
        free = [i for i in range(1, number_of) if holding[i] < largest] or [i for i in range(1, number_of) if holding[i] < limit]
        mass, remaining = sum([portions[i] for i in free]), spare
        for i in free:
            extra = min(limit - holding[i], max(1, remaining * portions[i] // mass), spare)
            holding[i] = holding[i] + extra
            spare = spare - extra
    return np.array(holding)


def bell_draw(own_key, dims, deviation, reach, shards=(), held_as=jnp.bfloat16):
    loudness = level_of(own_key, dims, shards, -0.22, 0.18) if shards else 1.0
    values = jax.random.normal(own_key, dims, jnp.float32) * deviation * loudness
    return jnp.minimum(jnp.maximum(values, -reach), reach).astype(held_as)


def setup_inputs(seed: int = 0) -> dict:
    key_of = jax.random.split(jax.random.key(seed), 15)
    inputs = bell_draw(key_of[0], (TOKENS, D), 1.0, 6.0, ((0, 32),))
    cotangent = bell_draw(key_of[1], (TOKENS, D), 1.0, 6.0, ((0, 32),))
    routes_keys = jax.random.split(jax.random.fold_in(key_of[2], 1), TOKENS // BLOCK)
    routes_turns = jax.random.permutation(jax.random.fold_in(key_of[2], 3), TOKENS // BLOCK)
    routes = jax.vmap(lambda own, number: deal_out(jax.random.fold_in(key_of[2], 2), own, number, BLOCK, EXPERTS, TOP, CAP, 1))(routes_keys, routes_turns).reshape((TOKENS, TOP))
    gain_attn = jnp.clip(1.0 + 0.1 * jax.random.normal(key_of[3], (D,), jnp.float32), 0.5, 1.5)
    w_qkv = bell_draw(key_of[4], (D, 3, HID), D ** -0.5, 0.125, ((0, 8), (2, 4)), jnp.float32)
    qkv_bias = bell_draw(key_of[5], (3, HEADS, HEAD_DIM), 0.1, 0.6, ((1, 4), (2, 8)), jnp.float32)
    w_out = bell_draw(key_of[6], (D, HID), (HID // 64) ** -0.5, 1.0, ((0, 8), (1, 4)), jnp.float32)
    gain_ffn = jnp.clip(1.0 + 0.1 * jax.random.normal(key_of[7], (D,), jnp.float32), 0.5, 1.5)
    router = bell_draw(key_of[8], (EXPERTS, D), (4 * D) ** -0.5, 0.0625, (), jnp.float32)
    shared_gate = bell_draw(key_of[9], (D,), D ** -0.5, 0.125, (), jnp.float32)
    expert_gate_up = bell_draw(key_of[10], (EXPERTS, 2, MOE_FF, D), D ** -0.5, 0.125, ((2, 4), (3, 8)), jnp.float32)
    expert_down = bell_draw(key_of[11], (EXPERTS, MOE_FF, D), (MOE_FF // 256 + 1) ** -0.5, 2.5, ((1, 4), (2, 8)), jnp.float32)
    shared_gate_up = bell_draw(key_of[12], (D, 2, SHARED_FF), D ** -0.5, 0.125, ((0, 8), (2, 4)), jnp.float32)
    shared_down = bell_draw(key_of[13], (D, SHARED_FF), (SHARED_FF // 4) ** -0.5, 0.15625, ((0, 8), (1, 4)), jnp.float32)
    return dict(inputs=inputs, cotangent=cotangent, routes=routes, gain_attn=gain_attn, w_qkv=w_qkv, qkv_bias=qkv_bias, w_out=w_out, gain_ffn=gain_ffn, router=router, shared_gate=shared_gate, expert_gate_up=expert_gate_up, expert_down=expert_down, shared_gate_up=shared_gate_up, shared_down=shared_down)


EPSILON = 1e-06
ROPE_BASE = 1000000.0
MASKED = -1000000000.0
HIGHEST = lax.Precision.HIGHEST

@jax.custom_vjp
def low(v):
    return lax.optimization_barrier(v.astype(jnp.bfloat16)).astype(jnp.float32)

@jax.custom_vjp
def low_back(v):
    return v

def low_keep(v):
    return (low(v), None)

def low_pass(kept, grad):
    return (grad,)

def back_keep(v):
    return (v, None)

def back_low(kept, grad):
    return (low(grad),)
low.defvjp(low_keep, low_pass)
low_back.defvjp(back_keep, back_low)

def block_layout(half_index):
    row_ids = jnp.arange(BLOCK, dtype=jnp.int32)
    half_len = PROMPT // 2
    offset = row_ids - half_len
    in_prompt = row_ids < half_len
    positions = jnp.where(in_prompt, half_index * half_len + row_ids, PROMPT + offset % CONT)
    segment = jnp.where(in_prompt, -1, half_index * (CONTS // 2) + offset // CONT)
    return (positions.astype(jnp.int32), segment.astype(jnp.int32))

def rotary(tensor_in, positions, direction):
    half_dim = tensor_in.shape[-1] // 2
    frequency = ROPE_BASE ** (-(jnp.arange(half_dim, dtype=jnp.float32) * 2.0 / tensor_in.shape[-1]))
    angles = positions.astype(jnp.float32)[:, None] * frequency[None, :]
    cosine = jnp.cos(angles)[:, None, :]
    sine_part = direction * jnp.sin(angles)[:, None, :]
    first_half = tensor_in[..., :half_dim]
    second_half = tensor_in[..., half_dim:]
    return jnp.concatenate([first_half * cosine - second_half * sine_part, second_half * cosine + first_half * sine_part], -1)

def allowed_mask(query_pos, query_seg, local_pos, local_seg):
    prompt_pos = jnp.arange(PROMPT, dtype=jnp.int32)
    continued = query_seg[:, None] >= 0
    prompt_part = continued | (prompt_pos[None, :] <= query_pos[:, None])
    local_part = continued & (local_seg[None, :] == query_seg[:, None]) & (local_pos[None, :] <= query_pos[:, None])
    return jnp.concatenate([prompt_part, local_part], 1)

def slot_table(block_routes):
    flat_routes = block_routes.reshape(-1)
    onehot = (flat_routes[:, None] == jnp.arange(EXPERTS, dtype=jnp.int32)[None, :]).astype(jnp.int32)
    earlier = jnp.cumsum(onehot, 0) - onehot
    rank_in = lax.optimization_barrier(jnp.sum(earlier * onehot, 1))
    slot_index = (flat_routes * CAP + rank_in).astype(jnp.int32)
    pair_token = (jnp.arange(flat_routes.shape[0], dtype=jnp.int32) // TOP).astype(jnp.int32)
    slot_owner = jnp.full((EXPERTS * CAP,), BLOCK, jnp.int32).at[slot_index].set(pair_token)
    return (slot_index, slot_owner)

def attend(queries, key_rows, value_rows, positions, segment):
    half_len = PROMPT // 2
    prompt_keys = jnp.concatenate([key_rows[:half_len], key_rows[BLOCK:BLOCK + half_len]], 0)
    prompt_values = jnp.concatenate([value_rows[:half_len], value_rows[BLOCK:BLOCK + half_len]], 0)
    scale_factor = queries.shape[-1] ** (-0.5)

    def one_block(first_row):
        query_rows = lax.dynamic_slice_in_dim(queries, first_row, QBLOCK, 0)
        key_all = jnp.concatenate([prompt_keys, lax.dynamic_slice_in_dim(key_rows, first_row, QBLOCK, 0)], 0)
        value_all = jnp.concatenate([prompt_values, lax.dynamic_slice_in_dim(value_rows, first_row, QBLOCK, 0)], 0)
        query_pos = lax.dynamic_slice_in_dim(positions, first_row, QBLOCK, 0)
        query_seg = lax.dynamic_slice_in_dim(segment, first_row, QBLOCK, 0)
        allowed = allowed_mask(query_pos, query_seg, query_pos, query_seg)
        scores = low_back(jnp.einsum('qhd,khd->hqk', query_rows, key_all, precision=HIGHEST) * scale_factor)
        scores = jnp.where(allowed[None], scores, MASKED)
        attn_probs = low(jax.nn.softmax(scores, -1))
        return jnp.einsum('hqk,khd->qhd', attn_probs, value_all, precision=HIGHEST)
    starts = jnp.arange(2 * BLOCK // QBLOCK, dtype=jnp.int32) * QBLOCK
    blocks = lax.map(jax.checkpoint(one_block), starts)
    return blocks.reshape(queries.shape)

def routed(rows_in, block_routes, gate_values, gate_up, down_rows):
    slot_index, slot_owner = slot_table(block_routes)
    padded = jnp.concatenate([rows_in, jnp.zeros((1, rows_in.shape[1]), jnp.float32)], 0)
    taken = padded[slot_owner].reshape(EXPERTS, CAP, rows_in.shape[1])
    pre_act = low_back(jnp.einsum('ecd,ejfd->ecjf', taken, gate_up, precision=HIGHEST))
    hidden = low(jax.nn.silu(pre_act[:, :, 0]) * pre_act[:, :, 1])
    result = low_back(jnp.einsum('ecf,efd->ecd', hidden, down_rows, precision=HIGHEST))
    slot_gate = jnp.zeros((EXPERTS * CAP,), jnp.float32).at[slot_index].set(gate_values.reshape(-1))
    weighted = result.reshape(EXPERTS * CAP, rows_in.shape[1]) * slot_gate[:, None]
    summed = jnp.zeros((BLOCK + 1, rows_in.shape[1]), jnp.float32).at[slot_owner].add(weighted)
    return summed[:BLOCK]

def group_forward(weights, row_data, group_routes):
    gain_attn, w_qkv, qkv_bias, w_out, gain_ffn, router, shared_gate, expert_gate_up, expert_down, shared_gate_up, shared_down = weights
    total_rows = row_data.shape[0]
    heads = qkv_bias.shape[1]
    first_pos, first_seg = block_layout(0)
    second_pos, second_seg = block_layout(1)
    positions = jnp.concatenate([first_pos, second_pos], 0)
    segment = jnp.concatenate([first_seg, second_seg], 0)
    normed_first = row_data * lax.rsqrt(lax.optimization_barrier(jnp.mean(row_data * row_data, -1, keepdims=True)) + EPSILON)
    first_in = low(normed_first * gain_attn)
    projected = jnp.einsum('td,djh->tjh', first_in, low(w_qkv), precision=HIGHEST) + low(qkv_bias).reshape(3, -1)
    projected = low_back(projected)
    queries = low(rotary(projected[:, 0].reshape(total_rows, heads, -1), positions, 1.0))
    key_rows = low(rotary(projected[:, 1].reshape(total_rows, heads, -1), positions, 1.0))
    value_rows = low(projected[:, 2].reshape(total_rows, heads, -1))
    attended = low(low_back(attend(queries, key_rows, value_rows, positions, segment))).reshape(total_rows, -1)
    branch = low_back(jnp.einsum('th,dh->td', attended, low(w_out), precision=HIGHEST))
    middle = row_data + branch
    normed_second = middle * lax.rsqrt(lax.optimization_barrier(jnp.mean(middle * middle, -1, keepdims=True)) + EPSILON)
    second_in = low(normed_second * gain_ffn)
    router_probs = jax.nn.softmax(jnp.einsum('td,ed->te', second_in, low(router), precision=HIGHEST), -1)
    gate_values = low(jnp.take_along_axis(router_probs, group_routes, 1))
    shared_scale = low(jax.nn.sigmoid(jnp.dot(second_in, low(shared_gate), precision=HIGHEST)))
    gate_up = low(expert_gate_up)
    down_rows = low(expert_down)
    routed_out = jnp.concatenate([routed(second_in[:BLOCK], group_routes[:BLOCK], gate_values[:BLOCK], gate_up, down_rows), routed(second_in[BLOCK:], group_routes[BLOCK:], gate_values[BLOCK:], gate_up, down_rows)], 0)
    shared_pre = low_back(jnp.einsum('td,djf->tjf', second_in, low(shared_gate_up), precision=HIGHEST))
    shared_hidden = low(jax.nn.silu(shared_pre[:, 0]) * shared_pre[:, 1])
    shared_result = low_back(jnp.einsum('tf,df->td', shared_hidden, low(shared_down), precision=HIGHEST))
    mixed = low_back(routed_out + shared_scale[:, None] * shared_result)
    return middle + mixed

def reference(inputs, cotangent, routes, gain_attn, w_qkv, qkv_bias, w_out, gain_ffn, router, shared_gate, expert_gate_up, expert_down, shared_gate_up, shared_down):
    floats = tuple((item.astype(jnp.float32) for item in (inputs, gain_attn, w_qkv, qkv_bias, w_out, gain_ffn, router, shared_gate, expert_gate_up, expert_down, shared_gate_up, shared_down)))
    groups = N_DP // 2
    grouped_routes = routes.reshape(groups, 2 * BLOCK, TOP)

    def forward(row_data, *weights):
        grouped = row_data.reshape(groups, 2 * BLOCK, row_data.shape[1])

        def one_group(paired):
            return group_forward(weights, paired[0], paired[1])
        outputs = lax.map(jax.checkpoint(one_group), (grouped, grouped_routes))
        return outputs.reshape(row_data.shape)
    layer_out, pullback = jax.vjp(forward, *floats)
    grads = pullback(cotangent.astype(jnp.float32))
    return (layer_out.astype(jnp.bfloat16), grads[0], grads[1], grads[2], grads[3], grads[4], grads[5], grads[6], grads[7], grads[8], grads[9], grads[10], grads[11])
```

```python
import jax
import jax.numpy as jnp
from jax import lax
from jax.sharding import PartitionSpec as P

TOP = 4
EXPERTS = 16
PROMPT = 2048
CONT = 256
CONTS = 4
QBLOCK = 512
BLOCK = 1536
CAP = 408


EPSILON = 1e-06
ROPE_BASE = 1000000.0
MASKED = -1000000000.0


def from_partner(value, axis, distance):
    mask = 2**distance
    pairs = [(source, source ^ mask) for source in range(lax.axis_size(axis))]
    return lax.ppermute(value, axis, pairs)


def block_layout(half_index):
    row_ids = jnp.arange(BLOCK, dtype=jnp.int32)
    half_len = PROMPT // 2
    offset = row_ids - half_len
    in_prompt = row_ids < half_len
    positions = jnp.where(in_prompt, half_index * half_len + row_ids, PROMPT + offset % CONT)
    segment = jnp.where(in_prompt, -1, half_index * (CONTS // 2) + offset // CONT)
    return (positions, segment)


def rotary(tensor_in, positions, direction):
    half_dim = tensor_in.shape[-1] // 2
    frequency = ROPE_BASE ** (
        -(jnp.arange(half_dim, dtype=jnp.float32) * 2.0 / tensor_in.shape[-1])
    )
    angles = positions.astype(jnp.float32)[:, None] * frequency[None, :]
    cosine = jnp.cos(angles)[:, None, :]
    sine_part = direction * jnp.sin(angles)[:, None, :]
    first_half = tensor_in[..., :half_dim]
    second_half = tensor_in[..., half_dim:]
    return jnp.concatenate(
        [
            first_half * cosine - second_half * sine_part,
            second_half * cosine + first_half * sine_part,
        ],
        -1,
    )


def allowed_mask(query_pos, query_seg, local_pos, local_seg):
    prompt_pos = jnp.arange(PROMPT, dtype=jnp.int32)
    continued = query_seg[:, None] >= 0
    prompt_part = continued | (prompt_pos[None, :] <= query_pos[:, None])
    local_part = (
        continued
        & (local_seg[None, :] == query_seg[:, None])
        & (local_pos[None, :] <= query_pos[:, None])
    )
    return jnp.concatenate([prompt_part, local_part], 1)


def expert_groups(dp_count, tensor_count):
    blocks = EXPERTS // tensor_count
    replicas = dp_count // blocks
    members = [
        [
            (i * replicas + g) * tensor_count + t
            for i in range(blocks)
            for t in range(tensor_count)
        ]
        for g in range(replicas)
    ]
    return (blocks, replicas, members)


def swap_groups(value, members):
    return lax.all_to_all(
        value, ("dp", "tensor"), split_axis=0, concat_axis=0, tiled=True, axis_index_groups=members
    )


def sum_over_tensor(value):
    count = lax.axis_size("tensor")
    pieces = lax.all_to_all(value, "tensor", split_axis=0, concat_axis=0, tiled=True)
    pieces = pieces.reshape((count, value.shape[0] // count) + value.shape[1:])
    return jnp.sum(pieces.astype(jnp.float32), 0)


def gather_expert(gate_up, down_rows, groups):
    blocks, replicas, members = groups
    dp_count = lax.axis_size("dp")
    tensor_count = lax.axis_size("tensor")
    hidden_part = down_rows.shape[1]
    width_part = down_rows.shape[2]
    packed = jnp.concatenate(
        [gate_up.astype(jnp.bfloat16), down_rows.astype(jnp.bfloat16)[:, None]], 1
    ).reshape(EXPERTS, 3 * hidden_part, width_part)
    own = swap_groups(packed, members)
    if replicas == 2:
        other = lax.ppermute(own, "dp", [(s, s ^ 1) for s in range(dp_count)])
        first = lax.axis_index("dp") % 2 == 0
        both = jnp.stack([jnp.where(first, own, other), jnp.where(first, other, own)])
    else:
        lines = [[i * replicas + g for g in range(replicas)] for i in range(blocks)]
        both = lax.all_gather(own, "dp", axis=0, tiled=False, axis_index_groups=lines)
    both = both.reshape(replicas, blocks, tensor_count, 3, hidden_part, width_part)
    both = jnp.transpose(both, (3, 2, 4, 1, 0, 5))
    return both.reshape(3, tensor_count * hidden_part, dp_count * width_part)


def return_expert_grads(grads, groups):
    blocks, replicas, members = groups
    dp_count = lax.axis_size("dp")
    tensor_count = lax.axis_size("tensor")
    hidden_part = grads.shape[1] // tensor_count
    width_part = grads.shape[2] // dp_count
    split = grads.reshape(3, tensor_count, hidden_part, blocks, replicas, width_part)
    split = jnp.transpose(split, (4, 3, 1, 0, 2, 5)).reshape(
        replicas, EXPERTS, 3 * hidden_part, width_part
    )
    if replicas == 2:
        first = lax.axis_index("dp") % 2 == 0
        own = jnp.where(first, split[0], split[1])
        other = jnp.where(first, split[1], split[0])
        back = lax.ppermute(other, "dp", [(s, s ^ 1) for s in range(dp_count)])
        summed = (own.astype(jnp.float32) + back.astype(jnp.float32)).astype(jnp.bfloat16)
    else:
        lines = [[i * replicas + g for g in range(replicas)] for i in range(blocks)]
        pieces = lax.all_to_all(
            split, "dp", split_axis=0, concat_axis=0, tiled=True, axis_index_groups=lines
        )
        summed = jnp.sum(pieces.astype(jnp.float32), 0).astype(jnp.bfloat16)
    shares = swap_groups(summed, members).astype(jnp.float32)
    shares = shares.reshape(EXPERTS, 3, hidden_part, width_part)
    return (shares[:, :2], shares[:, 2])


def normalize(row_data):
    factor = lax.rsqrt(jnp.mean(row_data * row_data, -1, keepdims=True) + EPSILON)
    return (row_data * factor, factor)


def norm_back(gradient, normed, factor, gain_vec):
    scaled = gradient * gain_vec
    return factor * (scaled - normed * jnp.mean(scaled * normed, -1, keepdims=True))


def silu_back(pre_act, gradient):
    gate_pre = pre_act[:, 0]
    up_pre = pre_act[:, 1]
    sigmoid_val = jax.nn.sigmoid(gate_pre)
    activated = gate_pre * sigmoid_val
    gate_part = gradient * up_pre * sigmoid_val * (1.0 + gate_pre * (1.0 - sigmoid_val))
    return jnp.stack([gate_part, gradient * activated], 1)


def local(
    inputs,
    cotangent,
    routes,
    gain_attn,
    w_qkv,
    qkv_bias,
    w_out,
    gain_ffn,
    router,
    shared_gate,
    expert_gate_up,
    expert_down,
    shared_gate_up,
    shared_down,
):
    tok_rows = inputs.shape[0]
    model_width = inputs.shape[1]
    dp_count = lax.axis_size("dp")
    tensor_count = lax.axis_size("tensor")
    row_start = lax.axis_index("tensor") * tok_rows
    groups = expert_groups(dp_count, tensor_count)
    half_index = lax.axis_index("dp") % 2
    positions, segment = block_layout(half_index)
    half_len = PROMPT // 2
    own_first = half_index == 0
    qkv_full, out_full, bias_full, shared_up_full, shared_down_full = (
        lax.all_gather(w_qkv.astype(jnp.bfloat16), "dp", axis=0, tiled=True),
        lax.all_gather(w_out.astype(jnp.bfloat16), "dp", axis=0, tiled=True),
        lax.all_gather(qkv_bias.astype(jnp.bfloat16), "dp", axis=2, tiled=True),
        lax.all_gather(shared_gate_up.astype(jnp.bfloat16), "dp", axis=0, tiled=True),
        lax.all_gather(shared_down.astype(jnp.bfloat16), "dp", axis=0, tiled=True),
    )
    expert_rows = gather_expert(expert_gate_up, expert_down, groups)
    heads_local = bias_full.shape[1]
    head_width = bias_full.shape[2]
    local_width = heads_local * head_width
    block_in = lax.all_gather(inputs, "tensor", axis=0, tiled=True)
    normed_first, factor_first = normalize(block_in.astype(jnp.float32))
    first_in = (normed_first * gain_attn).astype(jnp.bfloat16)
    projected = jnp.einsum("td,djh->tjh", first_in, qkv_full, preferred_element_type=jnp.float32)
    projected = projected + bias_full.astype(jnp.float32).reshape(3, local_width)
    queries = rotary(
        projected[:, 0].reshape(BLOCK, heads_local, head_width), positions, 1.0
    ).astype(jnp.bfloat16)
    key_block = rotary(
        projected[:, 1].reshape(BLOCK, heads_local, head_width), positions, 1.0
    ).astype(jnp.bfloat16)
    values = projected[:, 2].reshape(BLOCK, heads_local, head_width).astype(jnp.bfloat16)
    partner_keys, partner_values = from_partner((key_block[:half_len], values[:half_len]), "dp", 0)
    prompt_keys = jnp.where(
        own_first,
        jnp.concatenate([key_block[:half_len], partner_keys], 0),
        jnp.concatenate([partner_keys, key_block[:half_len]], 0),
    )
    prompt_values = jnp.where(
        own_first,
        jnp.concatenate([values[:half_len], partner_values], 0),
        jnp.concatenate([partner_values, values[:half_len]], 0),
    )
    scale_factor = head_width ** (-0.5)
    block_count = BLOCK // QBLOCK
    starts = jnp.arange(block_count, dtype=jnp.int32) * QBLOCK

    def block_scores(first_row):
        query_rows = lax.dynamic_slice_in_dim(queries, first_row, QBLOCK, 0)
        key_all = jnp.concatenate(
            [prompt_keys, lax.dynamic_slice_in_dim(key_block, first_row, QBLOCK, 0)], 0
        )
        value_all = jnp.concatenate(
            [prompt_values, lax.dynamic_slice_in_dim(values, first_row, QBLOCK, 0)], 0
        )
        query_pos = lax.dynamic_slice_in_dim(positions, first_row, QBLOCK, 0)
        query_seg = lax.dynamic_slice_in_dim(segment, first_row, QBLOCK, 0)
        allowed = allowed_mask(query_pos, query_seg, query_pos, query_seg)
        scores = (
            jnp.einsum("qhd,khd->hqk", query_rows, key_all, preferred_element_type=jnp.float32)
            * scale_factor
        )
        scores = jnp.where(allowed[None], scores, MASKED)
        return (scores, query_rows, key_all, value_all)

    def attend_block(first_row):
        scores, query_rows, key_all, value_all = block_scores(first_row)
        highest = jnp.max(scores, -1, keepdims=True)
        weights = jnp.exp(scores - highest)
        totals = jnp.sum(weights, -1, keepdims=True)
        attn_probs = (weights / totals).astype(jnp.bfloat16)
        attended = jnp.einsum(
            "hqk,khd->qhd", attn_probs, value_all, preferred_element_type=jnp.float32
        )
        return (attended, (highest + jnp.log(totals))[..., 0])

    attended, log_totals = lax.map(attend_block, starts)
    attended_b = attended.reshape(BLOCK, local_width).astype(jnp.bfloat16)
    attn_local = sum_over_tensor(
        jnp.einsum("th,dh->td", attended_b, out_full, preferred_element_type=jnp.float32).astype(
            jnp.bfloat16
        )
    )
    middle = inputs.astype(jnp.float32) + attn_local
    normed_second, factor_second = normalize(middle)
    second_local = (normed_second * gain_ffn).astype(jnp.bfloat16)
    second_in = lax.all_gather(second_local, "tensor", axis=0, tiled=True)
    grad_rows = lax.all_gather(cotangent, "tensor", axis=0, tiled=True)
    gate_rows = jnp.concatenate([router, shared_gate[None, :]], 0).astype(jnp.bfloat16)
    logits = jnp.einsum("ed,td->et", gate_rows, second_in, preferred_element_type=jnp.float32)
    router_probs = jax.nn.softmax(logits[:EXPERTS], 0)
    shared_prob = jax.nn.sigmoid(logits[EXPERTS])
    shared_scale = shared_prob.astype(jnp.bfloat16).astype(jnp.float32)
    gate_values = router_probs.astype(jnp.bfloat16)

    expert_ids = jnp.arange(EXPERTS, dtype=jnp.int32)
    named = jnp.any(routes.T[:, None, :] == expert_ids[None, :, None], 0)
    row_ids = jnp.arange(BLOCK, dtype=jnp.int32)
    before = (row_ids[:, None] < row_ids[None, :]).astype(jnp.bfloat16)
    rank_in = jnp.einsum(
        "et,ts->es", named.astype(jnp.bfloat16), before, preferred_element_type=jnp.float32
    ).astype(jnp.int32)
    share = -(-CAP // (8 * tensor_count)) * 8
    slots = EXPERTS * share
    slot_ids = jnp.arange(share, dtype=jnp.int32) + share * lax.axis_index("tensor")
    owned = named[:, None, :] & (rank_in[:, None, :] == slot_ids[None, :, None])
    pick = owned.astype(jnp.bfloat16).reshape(slots, BLOCK)
    slot_gate = jnp.sum(
        jnp.where(owned, gate_values[:, None, :], 0).astype(jnp.float32), -1
    ).reshape(slots, 1)
    members = groups[2]
    taken_send = jnp.einsum("mt,td->md", pick, second_in, preferred_element_type=jnp.float32)
    taken = swap_groups(
        taken_send.astype(jnp.bfloat16).reshape(EXPERTS, share, model_width), members
    ).reshape(slots, model_width)
    slot_cot = jnp.einsum("mt,td->md", pick, grad_rows, preferred_element_type=jnp.float32)
    result_grad = swap_groups(
        (slot_cot * slot_gate).astype(jnp.bfloat16).reshape(EXPERTS, share, model_width), members
    ).reshape(slots, model_width)
    slot_cot = slot_cot.astype(jnp.bfloat16)

    pre_act = jnp.einsum(
        "cd,jfd->cjf", taken, expert_rows[:2], preferred_element_type=jnp.float32
    )
    hidden = (jax.nn.silu(pre_act[:, 0]) * pre_act[:, 1]).astype(jnp.bfloat16)
    result = jnp.einsum("cf,fd->cd", hidden, expert_rows[2], preferred_element_type=jnp.float32)
    result_back = swap_groups(
        result.astype(jnp.bfloat16).reshape(EXPERTS, share, model_width), members
    ).reshape(slots, model_width)
    hidden_grad = jnp.einsum(
        "cd,fd->cf", result_grad, expert_rows[2], preferred_element_type=jnp.float32
    )
    pre_grad = silu_back(pre_act, hidden_grad).astype(jnp.bfloat16)
    rows_grad = jnp.einsum(
        "cjf,jfd->cd", pre_grad, expert_rows[:2], preferred_element_type=jnp.float32
    )
    rows_back = swap_groups(
        rows_grad.astype(jnp.bfloat16).reshape(EXPERTS, share, model_width), members
    ).reshape(slots, model_width)
    gate_up_part = jnp.einsum("cjf,cd->jfd", pre_grad, taken, preferred_element_type=jnp.float32)
    down_part = jnp.einsum("cf,cd->fd", hidden, result_grad, preferred_element_type=jnp.float32)
    expert_gate_up_grad, expert_down_grad = return_expert_grads(
        jnp.concatenate([gate_up_part.astype(jnp.bfloat16), down_part.astype(jnp.bfloat16)[None]], 0),
        groups,
    )

    shared_pre = jnp.einsum(
        "td,djf->tjf", second_in, shared_up_full, preferred_element_type=jnp.float32
    )
    shared_hidden = (jax.nn.silu(shared_pre[:, 0]) * shared_pre[:, 1]).astype(jnp.bfloat16)
    shared_result = jnp.einsum(
        "tf,df->td", shared_hidden, shared_down_full, preferred_element_type=jnp.float32
    )
    gated_pick = pick * slot_gate.astype(jnp.bfloat16)
    combined = jnp.einsum("mt,md->td", gated_pick, result_back, preferred_element_type=jnp.float32)
    mixed_part = combined + shared_scale[:, None] * shared_result
    mixed_local = sum_over_tensor(mixed_part.astype(jnp.bfloat16))
    layer_out = (middle + mixed_local).astype(jnp.bfloat16)

    slot_grad = jnp.sum(slot_cot.astype(jnp.float32) * result_back.astype(jnp.float32), -1)
    prob_grad = jnp.sum(jnp.where(owned, slot_grad.reshape(EXPERTS, share, 1), 0.0), 1)
    logit_grad = router_probs * (prob_grad - jnp.sum(router_probs * prob_grad, 0, keepdims=True))
    grad_rows_f = grad_rows.astype(jnp.float32)
    shared_scale_grad = jnp.sum(grad_rows_f * shared_result, -1)
    shared_logit_grad = shared_scale_grad * shared_prob * (1.0 - shared_prob)
    logit_grads = jnp.concatenate([logit_grad, shared_logit_grad[None, :]], 0).astype(jnp.bfloat16)
    gate_rows_part = jnp.einsum(
        "et,td->ed", logit_grads, second_in, preferred_element_type=jnp.float32
    )
    shared_result_grad = (shared_scale[:, None] * grad_rows_f).astype(jnp.bfloat16)
    shared_hidden_grad = jnp.einsum(
        "td,df->tf", shared_result_grad, shared_down_full, preferred_element_type=jnp.float32
    )
    shared_pre_grad = silu_back(shared_pre, shared_hidden_grad).astype(jnp.bfloat16)
    shared_down_part = jnp.einsum(
        "td,tf->df", shared_result_grad, shared_hidden, preferred_element_type=jnp.float32
    )
    shared_up_part = jnp.einsum(
        "td,tjf->djf", second_in, shared_pre_grad, preferred_element_type=jnp.float32
    )
    grad_second = jnp.einsum(
        "tjf,djf->td", shared_pre_grad, shared_up_full, preferred_element_type=jnp.float32
    )
    grad_second = grad_second + jnp.einsum(
        "et,ed->td", logit_grads, gate_rows, preferred_element_type=jnp.float32
    )
    grad_second = grad_second + jnp.einsum(
        "mt,md->td", pick, rows_back, preferred_element_type=jnp.float32
    )
    second_grad = sum_over_tensor(grad_second.astype(jnp.bfloat16))
    gain_ffn_part = jnp.sum(second_grad * normed_second, 0)
    middle_grad = cotangent.astype(jnp.float32) + norm_back(
        second_grad, normed_second, factor_second, gain_ffn
    )
    branch_grad = lax.all_gather(middle_grad.astype(jnp.bfloat16), "tensor", axis=0, tiled=True)
    attended_grad = jnp.einsum(
        "td,dh->th", branch_grad, out_full, preferred_element_type=jnp.float32
    ).astype(jnp.bfloat16)
    w_out_part = jnp.einsum(
        "td,th->dh", branch_grad, attended_b, preferred_element_type=jnp.float32
    )
    attended_grad = attended_grad.reshape(block_count, QBLOCK, heads_local, head_width)

    def attend_back(running, scanned):
        key_sums, value_sums = running
        first_row, log_total, out_grad = scanned
        scores, query_rows, key_all, value_all = block_scores(first_row)
        attn_probs = jnp.exp(scores - log_total[..., None])
        probs_b = attn_probs.astype(jnp.bfloat16)
        attn_prob_grad = jnp.einsum(
            "qhd,khd->hqk", out_grad, value_all, preferred_element_type=jnp.float32
        )
        score_grad = attn_probs * (
            attn_prob_grad - jnp.sum(attn_probs * attn_prob_grad, -1, keepdims=True)
        )
        score_grad = score_grad.astype(jnp.bfloat16)
        query_grad = (
            jnp.einsum("hqk,khd->qhd", score_grad, key_all, preferred_element_type=jnp.float32)
            * scale_factor
        )
        key_grad = (
            jnp.einsum("hqk,qhd->khd", score_grad, query_rows, preferred_element_type=jnp.float32)
            * scale_factor
        )
        value_grad = jnp.einsum(
            "hqk,qhd->khd", probs_b, out_grad, preferred_element_type=jnp.float32
        )
        running = (key_sums + key_grad[:PROMPT], value_sums + value_grad[:PROMPT])
        return (running, (query_grad, key_grad[PROMPT:], value_grad[PROMPT:]))

    empty_prompt = jnp.zeros((PROMPT, heads_local, head_width), jnp.float32)
    (key_sums, value_sums), (query_grads, local_key_grads, local_value_grads) = lax.scan(
        attend_back, (empty_prompt, empty_prompt), (starts, log_totals, attended_grad)
    )
    own_keys = jnp.where(own_first, key_sums[:half_len], key_sums[half_len:])
    other_keys = jnp.where(own_first, key_sums[half_len:], key_sums[:half_len])
    own_values = jnp.where(own_first, value_sums[:half_len], value_sums[half_len:])
    other_values = jnp.where(own_first, value_sums[half_len:], value_sums[:half_len])
    back_keys, back_values = (
        from_partner(other_keys.astype(jnp.bfloat16), "dp", 0).astype(other_keys.dtype),
        from_partner(other_values.astype(jnp.bfloat16), "dp", 0).astype(other_values.dtype),
    )
    key_grad_rows = local_key_grads.reshape(BLOCK, heads_local, head_width)
    key_grad_rows = jnp.concatenate(
        [key_grad_rows[:half_len] + own_keys + back_keys, key_grad_rows[half_len:]], 0
    )
    value_grad_rows = local_value_grads.reshape(BLOCK, heads_local, head_width)
    value_grad_rows = jnp.concatenate(
        [value_grad_rows[:half_len] + own_values + back_values, value_grad_rows[half_len:]], 0
    )
    query_grad_rows = query_grads.reshape(BLOCK, heads_local, head_width)
    qkv_grad = (
        jnp.stack(
            [
                rotary(query_grad_rows, positions, -1.0),
                rotary(key_grad_rows, positions, -1.0),
                value_grad_rows,
            ],
            1,
        )
        .reshape(BLOCK, 3, local_width)
        .astype(jnp.bfloat16)
    )
    bias_part = jnp.sum(qkv_grad.astype(jnp.float32), 0).reshape(3, heads_local, head_width)
    w_qkv_part = jnp.einsum("td,tjh->djh", first_in, qkv_grad, preferred_element_type=jnp.float32)
    first_grad_part = jnp.einsum(
        "tjh,djh->td", qkv_grad, qkv_full, preferred_element_type=jnp.float32
    )
    gain_attn_part = jnp.sum(first_grad_part * normed_first, 0)
    first_grad = sum_over_tensor(first_grad_part.astype(jnp.bfloat16))
    gate_share = lax.psum_scatter(
        jnp.concatenate([gate_rows_part, gain_ffn_part[None, :]], 0),
        ("dp", "tensor"),
        scatter_dimension=1,
        tiled=True,
    )
    gain_attn_share = lax.psum_scatter(
        gain_attn_part, ("dp", "tensor"), scatter_dimension=0, tiled=True
    )
    normed_local = lax.dynamic_slice_in_dim(normed_first, row_start, tok_rows, 0)
    factor_local = lax.dynamic_slice_in_dim(factor_first, row_start, tok_rows, 0)
    input_grad = middle_grad + norm_back(first_grad, normed_local, factor_local, gain_attn)
    summed = (
        lax.psum_scatter(
            w_qkv_part.astype(jnp.bfloat16), "dp", scatter_dimension=0, tiled=True
        ).astype(jnp.float32),
        lax.psum_scatter(
            w_out_part.astype(jnp.bfloat16), "dp", scatter_dimension=0, tiled=True
        ).astype(jnp.float32),
        lax.psum_scatter(
            bias_part.astype(jnp.bfloat16), "dp", scatter_dimension=2, tiled=True
        ).astype(jnp.float32),
        lax.psum_scatter(
            shared_up_part.astype(jnp.bfloat16), "dp", scatter_dimension=0, tiled=True
        ).astype(jnp.float32),
        lax.psum_scatter(
            shared_down_part.astype(jnp.bfloat16), "dp", scatter_dimension=0, tiled=True
        ).astype(jnp.float32),
    )
    return (
        layer_out,
        input_grad,
        gain_attn_share,
        summed[0],
        summed[2],
        summed[1],
        gate_share[EXPERTS + 1],
        gate_share[:EXPERTS],
        gate_share[EXPERTS],
        expert_gate_up_grad,
        expert_down_grad,
        summed[3],
        summed[4],
    )


def solution(mesh):
    return jax.shard_map(
        local,
        mesh=mesh,
        in_specs=(
            P(("dp", "tensor"), None),
            P(("dp", "tensor"), None),
            P("dp", None),
            P(),
            P("dp", None, "tensor"),
            P(None, "tensor", "dp"),
            P("dp", "tensor"),
            P(),
            P(),
            P(),
            P(None, None, "tensor", "dp"),
            P(None, "tensor", "dp"),
            P("dp", None, "tensor"),
            P("dp", "tensor"),
        ),
        out_specs=(
            P(("dp", "tensor"), None),
            P(("dp", "tensor"), None),
            P(("dp", "tensor")),
            P("dp", None, "tensor"),
            P(None, "tensor", "dp"),
            P("dp", "tensor"),
            P(("dp", "tensor")),
            P(None, ("dp", "tensor")),
            P(("dp", "tensor")),
            P(None, None, "tensor", "dp"),
            P(None, "tensor", "dp"),
            P("dp", None, "tensor"),
            P("dp", "tensor"),
        ),
        check_vma=False,
    )
```

```python
import jax
import jax.numpy as jnp
from jax import lax
from jax.experimental import pallas as pl
from jax.experimental.pallas import tpu as pltpu
from jax.sharding import PartitionSpec as P

TOP = 4
EXPERTS = 16
PROMPT = 2048
CONT = 256
CONTS = 4
BLOCK = 1536
CAP = 408
TILE = 256
HALF = PROMPT // 2


EPSILON = 1e-06
ROPE_BASE = 1000000.0
MASKED = -1000000000.0


def from_partner(value, axis, distance):
    mask = 2**distance
    pairs = [(source, source ^ mask) for source in range(lax.axis_size(axis))]
    return lax.ppermute(value, axis, pairs)


def rope_tables(half_index, head_width):
    row_ids = jnp.arange(BLOCK, dtype=jnp.int32)
    offset = row_ids - HALF
    positions = jnp.where(row_ids < HALF, half_index * HALF + row_ids, PROMPT + offset % CONT)
    half_dim = head_width // 2
    lanes = jnp.arange(head_width, dtype=jnp.int32)
    frequency = ROPE_BASE ** (-((lanes % half_dim).astype(jnp.float32) * 2.0 / head_width))
    angles = positions.astype(jnp.float32)[:, None] * frequency[None, :]
    sign = jnp.where(lanes < half_dim, -1.0, 1.0).astype(jnp.float32)
    return (jnp.cos(angles), jnp.sin(angles) * sign[None, :])


def rotate_kernel(projected_ref, bias_ref, cosine_ref, sine_ref, query_ref, key_ref, value_ref):
    width = query_ref.shape[1]
    head_width = cosine_ref.shape[1]
    cosine = cosine_ref[...]
    sine = sine_ref[...]
    for part, out_ref in ((0, query_ref), (1, key_ref)):
        for head in range(width // head_width):
            low = head * head_width
            cols = pl.ds(part * width + low, head_width)
            rows = projected_ref[:, cols] + bias_ref[:, cols]
            turned = rows * cosine + pltpu.roll(rows, head_width // 2, 1) * sine
            out_ref[:, pl.ds(low, head_width)] = turned.astype(jnp.bfloat16)
    cols = pl.ds(2 * width, width)
    value_ref[...] = (projected_ref[:, cols] + bias_ref[:, cols]).astype(jnp.bfloat16)


def rotate_rows(projected, bias, cosine, sine):
    rows, width3 = projected.shape
    width = width3 // 3
    head_width = cosine.shape[1]
    out = jax.ShapeDtypeStruct((rows, width), jnp.bfloat16)
    row_block = lambda cols: pl.BlockSpec((TILE, cols), lambda i: (i, 0))
    return pl.pallas_call(
        rotate_kernel,
        grid=(rows // TILE,),
        in_specs=[
            row_block(width3),
            pl.BlockSpec((1, width3), lambda i: (0, 0)),
            row_block(head_width),
            row_block(head_width),
        ],
        out_specs=[row_block(width)] * 3,
        out_shape=[out] * 3,
        name="rotate_rows",
    )(projected, bias, cosine, sine)


def dot_nt(left, right):
    return lax.dot_general(
        left, right, (((1,), (1,)), ((), ())), preferred_element_type=jnp.float32
    )


def dot_nn(left, right):
    return lax.dot_general(
        left, right, (((1,), (0,)), ((), ())), preferred_element_type=jnp.float32
    )


def flip(value):
    return value.astype(jnp.float32).T


def own_limit(tile, keys, columns):
    row_ids = lax.broadcasted_iota(jnp.int32, (keys, columns), 0)
    col_ids = lax.broadcasted_iota(jnp.int32, (keys, columns), 1)
    start = jnp.where(tile < HALF // TILE, tile * TILE, HALF)
    return row_ids <= col_ids + start


def attend_kernel(
    half_ref, query_ref, key_ref, value_ref, far_key_ref, far_value_ref,
    near_key_ref, near_value_ref, out_ref, log_ref,
    value_flip, far_flip, peak_ref, total_ref, sum_ref,
):
    tile = pl.program_id(1)
    continued = tile >= HALF // TILE
    scale = key_ref.shape[1] ** (-0.5)

    @pl.when(tile == 0)
    def _():
        value_flip[...] = flip(value_ref[...]).astype(jnp.bfloat16)
        far_flip[...] = flip(far_value_ref[...]).astype(jnp.bfloat16)

    query = query_ref[...]
    scores = dot_nt(key_ref[...], query)
    scores = jnp.where(own_limit(tile, HALF, TILE), scores, MASKED)
    peak = jnp.max(scores, 0, keepdims=True)
    weights = jnp.exp((scores - peak) * scale)
    peak_ref[...] = peak
    total_ref[...] = jnp.sum(weights, 0, keepdims=True)
    sum_ref[...] = dot_nn(value_flip[...], weights.astype(jnp.bfloat16))

    def update(scores, flipped):
        old = peak_ref[...]
        peak = jnp.maximum(old, jnp.max(scores, 0, keepdims=True))
        shrink = jnp.exp((old - peak) * scale)
        weights = jnp.exp((scores - peak) * scale)
        peak_ref[...] = peak
        total_ref[...] = total_ref[...] * shrink + jnp.sum(weights, 0, keepdims=True)
        sum_ref[...] = sum_ref[...] * shrink + dot_nn(flipped, weights.astype(jnp.bfloat16))

    @pl.when(continued | (half_ref[0] == 1))
    def _():
        update(dot_nt(far_key_ref[...], query), far_flip[...])

    @pl.when(continued)
    def _():
        scores = dot_nt(near_key_ref[...], query)
        scores = jnp.where(own_limit(0, TILE, TILE), scores, MASKED)
        update(scores, flip(near_value_ref[...]).astype(jnp.bfloat16))

    total = total_ref[...]
    out_ref[...] = (sum_ref[...] / total).T.astype(jnp.bfloat16)
    log_ref[...] = jnp.broadcast_to(peak_ref[...] * scale + jnp.log(total), log_ref.shape)


def attend_specs(head_width):
    tile_block = pl.BlockSpec((TILE, head_width), lambda h, i, half: (i, h))
    half_block = pl.BlockSpec((HALF, head_width), lambda h, i, half: (0, h))
    log_block = pl.BlockSpec((8, TILE), lambda h, i, half: (h, i))
    return (tile_block, half_block, log_block)


def attend(half, queries, keys, values, far_keys, far_values, head_width):
    rows, width = queries.shape
    heads = width // head_width
    tile_block, half_block, log_block = attend_specs(head_width)
    return pl.pallas_call(
        attend_kernel,
        grid_spec=pltpu.PrefetchScalarGridSpec(
            num_scalar_prefetch=1,
            grid=(heads, rows // TILE),
            in_specs=[tile_block] + [half_block] * 4 + [tile_block] * 2,
            out_specs=[tile_block, log_block],
            scratch_shapes=[
                pltpu.VMEM((head_width, HALF), jnp.bfloat16),
                pltpu.VMEM((head_width, HALF), jnp.bfloat16),
                pltpu.VMEM((1, TILE), jnp.float32),
                pltpu.VMEM((1, TILE), jnp.float32),
                pltpu.VMEM((head_width, TILE), jnp.float32),
            ],
        ),
        out_shape=[
            jax.ShapeDtypeStruct((rows, width), jnp.bfloat16),
            jax.ShapeDtypeStruct((8 * heads, rows), jnp.float32),
        ],
        name="attend",
    )(half, queries, keys, values, far_keys, far_values, keys, values)


def attend_back_kernel(
    half_ref, query_ref, key_ref, value_ref, far_key_ref, far_value_ref,
    near_key_ref, near_value_ref, out_ref, log_ref, grad_ref, cosine_ref, sine_ref,
    query_grad_ref, key_grad_ref, value_grad_ref, far_key_grad_ref, far_value_grad_ref,
    near_key_grad_ref, near_value_grad_ref,
    key_flip, far_flip, sum_ref,
):
    tile = pl.program_id(1)
    continued = tile >= HALF // TILE
    head_width = key_ref.shape[1]
    scale = head_width ** (-0.5)

    @pl.when(tile == 0)
    def _():
        key_flip[...] = flip(key_ref[...]).astype(jnp.bfloat16)
        far_flip[...] = flip(far_key_ref[...]).astype(jnp.bfloat16)
        for ref in (key_grad_ref, value_grad_ref, far_key_grad_ref, far_value_grad_ref):
            ref[...] = jnp.zeros(ref.shape, jnp.float32)

    query = query_ref[...]
    grad = grad_ref[...]
    product = grad.astype(jnp.float32) * out_ref[...].astype(jnp.float32)
    inner = jnp.sum(product.T, 0, keepdims=True)
    log_total = log_ref[0:1, :]

    def block(keys, values, allowed):
        exponent = dot_nt(keys, query) * scale - log_total
        if allowed is not None:
            exponent = jnp.where(allowed, exponent, MASKED)
        probs = jnp.exp(exponent)
        score_grad = (probs * (dot_nt(values, grad) - inner)).astype(jnp.bfloat16)
        return (score_grad, dot_nn(score_grad, query) * scale, dot_nn(probs.astype(jnp.bfloat16), grad))

    score_grad, key_part, value_part = block(
        key_ref[...], value_ref[...], own_limit(tile, HALF, TILE)
    )
    key_grad_ref[...] += key_part
    value_grad_ref[...] += value_part
    sum_ref[...] = dot_nn(key_flip[...], score_grad)

    @pl.when(continued | (half_ref[0] == 1))
    def _():
        score_grad, key_part, value_part = block(far_key_ref[...], far_value_ref[...], None)
        far_key_grad_ref[...] += key_part
        far_value_grad_ref[...] += value_part
        sum_ref[...] += dot_nn(far_flip[...], score_grad)

    @pl.when(continued)
    def _():
        near_key = near_key_ref[...]
        score_grad, key_part, value_part = block(
            near_key, near_value_ref[...], own_limit(0, TILE, TILE)
        )
        near_key_grad_ref[...] = key_part
        near_value_grad_ref[...] = value_part
        sum_ref[...] += dot_nn(flip(near_key).astype(jnp.bfloat16), score_grad)

    rows = sum_ref[...].T * scale
    turned = rows * cosine_ref[...] - pltpu.roll(rows, head_width // 2, 1) * sine_ref[...]
    query_grad_ref[...] = turned.astype(jnp.bfloat16)


def attend_back(
    half, queries, keys, values, far_keys, far_values, attended, log_totals, grad, cosine, sine
):
    rows, width = queries.shape
    head_width = cosine.shape[1]
    heads = width // head_width
    tile_block, half_block, log_block = attend_specs(head_width)
    table_block = pl.BlockSpec((TILE, head_width), lambda h, i, half: (i, 0))
    near_block = pl.BlockSpec(
        (TILE, head_width), lambda h, i, half: (jnp.maximum(i - HALF // TILE, 0), h)
    )
    half_out = jax.ShapeDtypeStruct((HALF, width), jnp.float32)
    near_out = jax.ShapeDtypeStruct((rows - HALF, width), jnp.float32)
    return pl.pallas_call(
        attend_back_kernel,
        grid_spec=pltpu.PrefetchScalarGridSpec(
            num_scalar_prefetch=1,
            grid=(heads, rows // TILE),
            in_specs=[tile_block]
            + [half_block] * 4
            + [tile_block] * 3
            + [log_block, tile_block, table_block, table_block],
            out_specs=[tile_block] + [half_block] * 4 + [near_block] * 2,
            scratch_shapes=[
                pltpu.VMEM((head_width, HALF), jnp.bfloat16),
                pltpu.VMEM((head_width, HALF), jnp.bfloat16),
                pltpu.VMEM((head_width, TILE), jnp.float32),
            ],
        ),
        out_shape=[jax.ShapeDtypeStruct((rows, width), jnp.bfloat16)]
        + [half_out] * 4
        + [near_out] * 2,
        name="attend_back",
    )(
        half, queries, keys, values, far_keys, far_values, keys, values,
        attended, log_totals, grad, cosine, sine,
    )


def join_kernel(
    query_ref, key_ref, back_key_ref, near_key_ref, value_ref, back_value_ref, near_value_ref,
    cosine_ref, sine_ref, out_ref, sum_ref,
):
    tile = pl.program_id(0)
    width = query_ref.shape[1]
    head_width = cosine_ref.shape[1]
    prompt = tile < HALF // TILE
    cosine = cosine_ref[...]
    sine = sine_ref[...]

    @pl.when(tile == 0)
    def _():
        sum_ref[...] = jnp.zeros(sum_ref.shape, jnp.float32)

    out_ref[:, 0:width] = query_ref[...]
    keys = jnp.where(
        prompt, key_ref[...] + back_key_ref[...].astype(jnp.float32), near_key_ref[...]
    )
    for head in range(width // head_width):
        low = head * head_width
        rows = keys[:, low : low + head_width]
        turned = rows * cosine - pltpu.roll(rows, head_width // 2, 1) * sine
        out_ref[:, pl.ds(width + low, head_width)] = turned.astype(jnp.bfloat16)
    values = jnp.where(
        prompt, value_ref[...] + back_value_ref[...].astype(jnp.float32), near_value_ref[...]
    )
    out_ref[:, 2 * width : 3 * width] = values.astype(jnp.bfloat16)
    sum_ref[...] += jnp.sum(out_ref[...].astype(jnp.float32), 0, keepdims=True)


def join_grads(query_grad, key_grad, back_key, near_key, value_grad, back_value, near_value, cosine, sine):
    rows, width = query_grad.shape
    last = HALF // TILE - 1
    head_width = cosine.shape[1]
    row_block = lambda cols: pl.BlockSpec((TILE, cols), lambda i: (i, 0))
    half_block = pl.BlockSpec((TILE, width), lambda i: (jnp.minimum(i, last), 0))
    near_block = pl.BlockSpec((TILE, width), lambda i: (jnp.maximum(i - last - 1, 0), 0))
    return pl.pallas_call(
        join_kernel,
        grid=(rows // TILE,),
        in_specs=[row_block(width)]
        + [half_block, half_block, near_block] * 2
        + [row_block(head_width)] * 2,
        out_specs=[row_block(3 * width), pl.BlockSpec((1, 3 * width), lambda i: (0, 0))],
        out_shape=[
            jax.ShapeDtypeStruct((rows, 3 * width), jnp.bfloat16),
            jax.ShapeDtypeStruct((1, 3 * width), jnp.float32),
        ],
        name="join_grads",
    )(query_grad, key_grad, back_key, near_key, value_grad, back_value, near_value, cosine, sine)


def expert_groups(dp_count, tensor_count):
    blocks = EXPERTS // tensor_count
    replicas = dp_count // blocks
    members = [
        [
            (i * replicas + g) * tensor_count + t
            for i in range(blocks)
            for t in range(tensor_count)
        ]
        for g in range(replicas)
    ]
    return (blocks, replicas, members)


def swap_groups(value, members):
    return lax.all_to_all(
        value, ("dp", "tensor"), split_axis=0, concat_axis=0, tiled=True, axis_index_groups=members
    )


def choose(value, index, axis):
    return lax.dynamic_index_in_dim(value, index, axis, keepdims=False)


def sum_over_tensor(value):
    rank = lax.axis_index("tensor")
    count = lax.axis_size("tensor")
    if count != 4:
        pieces = lax.all_to_all(value, "tensor", split_axis=0, concat_axis=0, tiled=True)
        pieces = pieces.reshape((count, value.shape[0] // count) + value.shape[1:])
        return jnp.sum(pieces.astype(jnp.float32), 0)
    low = rank % 2
    high = rank // 2
    rows = value.shape[0] // 8
    split = value.reshape((2, 2, 2, rows) + value.shape[1:])
    first = split[:, :, 0]
    second = split[:, :, 1]
    first_in = from_partner(choose(first, 1 - low, 1), "tensor", 0)
    second_in = from_partner(choose(second, 1 - high, 0), "tensor", 1)
    first_sum = choose(first, low, 1).astype(jnp.float32) + first_in.astype(jnp.float32)
    second_sum = choose(second, high, 0).astype(jnp.float32) + second_in.astype(jnp.float32)
    first_far = from_partner(choose(first_sum, 1 - high, 0).astype(jnp.bfloat16), "tensor", 1)
    second_far = from_partner(choose(second_sum, 1 - low, 0).astype(jnp.bfloat16), "tensor", 0)
    return jnp.concatenate(
        [
            choose(first_sum, high, 0) + first_far.astype(jnp.float32),
            choose(second_sum, low, 0) + second_far.astype(jnp.float32),
        ],
        0,
    )


def gather_over_tensor(value):
    rank = lax.axis_index("tensor")
    if lax.axis_size("tensor") != 4:
        return lax.all_gather(value, "tensor", axis=0, tiled=True)
    rows = value.shape[0]
    half = rows // 2
    first = value[:half]
    second = value[half:]
    first_low = from_partner(first, "tensor", 0)
    second_high = from_partner(second, "tensor", 1)
    first_high = from_partner(first, "tensor", 1)
    second_low = from_partner(second, "tensor", 0)
    first_both = from_partner(first_low, "tensor", 1)
    second_both = from_partner(second_high, "tensor", 0)
    out = jnp.zeros((4 * rows,) + value.shape[1:], value.dtype)
    for mask, one, two in (
        (0, first, second),
        (1, first_low, second_low),
        (2, first_high, second_high),
        (3, first_both, second_both),
    ):
        start = (rank ^ mask) * rows
        out = lax.dynamic_update_slice_in_dim(out, one, start, 0)
        out = lax.dynamic_update_slice_in_dim(out, two, start + half, 0)
    return out


def gather_expert(shard, parts, groups):
    blocks, replicas, members = groups
    dp_count = lax.axis_size("dp")
    tensor_count = lax.axis_size("tensor")
    hidden_part = shard.shape[1] // parts
    width_part = shard.shape[2]
    own = swap_groups(shard, members)
    if replicas == 2:
        far = lax.ppermute(own, "dp", [(s, s ^ 1) for s in range(dp_count)])
        parity = lax.axis_index("dp") % 2
        shape = (blocks, tensor_count, parts, hidden_part, width_part)
        own = jnp.transpose(own.reshape(shape), (2, 1, 3, 0, 4))[..., None, :]
        far = jnp.transpose(far.reshape(shape), (2, 1, 3, 0, 4))[..., None, :]
        places = jnp.arange(2, dtype=jnp.int32)[:, None]
        both = jnp.where(places == parity, own, far)
    else:
        lines = [[i * replicas + g for g in range(replicas)] for i in range(blocks)]
        both = lax.all_gather(own, "dp", axis=0, tiled=False, axis_index_groups=lines)
        both = both.reshape(replicas, blocks, tensor_count, parts, hidden_part, width_part)
        both = jnp.transpose(both, (3, 2, 4, 1, 0, 5))
    return both.reshape(parts * tensor_count * hidden_part, dp_count * width_part)


def return_expert_grads(grads, parts, groups):
    blocks, replicas, members = groups
    dp_count = lax.axis_size("dp")
    tensor_count = lax.axis_size("tensor")
    hidden_part = grads.shape[0] // (parts * tensor_count)
    width_part = grads.shape[1] // dp_count
    split = grads.reshape(parts, tensor_count, hidden_part, blocks, replicas, width_part)
    shape = (EXPERTS, parts * hidden_part, width_part)
    if replicas == 2:
        parity = lax.axis_index("dp") % 2
        own = jnp.transpose(choose(split, parity, 4), (3, 1, 0, 2, 4)).reshape(shape)
        far = jnp.transpose(choose(split, 1 - parity, 4), (3, 1, 0, 2, 4)).reshape(shape)
        back = lax.ppermute(far, "dp", [(s, s ^ 1) for s in range(dp_count)])
        summed = (own.astype(jnp.float32) + back.astype(jnp.float32)).astype(jnp.bfloat16)
    else:
        split = jnp.transpose(split, (4, 3, 1, 0, 2, 5)).reshape((replicas,) + shape)
        lines = [[i * replicas + g for g in range(replicas)] for i in range(blocks)]
        pieces = lax.all_to_all(
            split, "dp", split_axis=0, concat_axis=0, tiled=True, axis_index_groups=lines
        )
        summed = jnp.sum(pieces.astype(jnp.float32), 0).astype(jnp.bfloat16)
    return swap_groups(summed, members)


def sum_over_all(value, groups):
    blocks, replicas, members = groups
    dp_count = lax.axis_size("dp")
    if replicas != 2:
        share = lax.psum_scatter(value, ("dp", "tensor"), scatter_dimension=0, tiled=True)
        return share.reshape(value.shape[1:])
    parity = lax.axis_index("dp") % 2
    split = value.reshape((blocks, 2, EXPERTS // blocks) + value.shape[1:])
    far = from_partner(choose(split, 1 - parity, 1), "dp", 0)
    pieces = choose(split, parity, 1) + far
    return jnp.sum(swap_groups(pieces.reshape((EXPERTS,) + value.shape[1:]), members), 0)


def normalize(row_data):
    factor = lax.rsqrt(jnp.mean(row_data * row_data, -1, keepdims=True) + EPSILON)
    return (row_data * factor, factor)


def norm_back(gradient, normed, factor, gain_vec):
    scaled = gradient * gain_vec
    return factor * (scaled - normed * jnp.mean(scaled * normed, -1, keepdims=True))


def silu_back(pre_act, gradient):
    half = pre_act.shape[1] // 2
    gate_pre = pre_act[:, :half]
    up_pre = pre_act[:, half:]
    sigmoid_val = jax.nn.sigmoid(gate_pre)
    activated = gate_pre * sigmoid_val
    gate_part = gradient * up_pre * sigmoid_val * (1.0 + gate_pre * (1.0 - sigmoid_val))
    return jnp.concatenate([gate_part, gradient * activated], 1)


def silu_up(pre_act):
    half = pre_act.shape[1] // 2
    return (jax.nn.silu(pre_act[:, :half]) * pre_act[:, half:]).astype(jnp.bfloat16)


def matmul(spec, left, right):
    return jnp.einsum(spec, left, right, preferred_element_type=jnp.float32)


def bf16(value):
    return value.astype(jnp.bfloat16)


def local(
    inputs,
    cotangent,
    routes,
    gain_attn,
    w_qkv,
    qkv_bias,
    w_out,
    gain_ffn,
    router,
    shared_gate,
    expert_gate_up,
    expert_down,
    shared_gate_up,
    shared_down,
):
    scope = jax.named_scope
    tok_rows, model_width = inputs.shape
    dp_count = lax.axis_size("dp")
    tensor_count = lax.axis_size("tensor")
    row_start = lax.axis_index("tensor") * tok_rows
    groups = expert_groups(dp_count, tensor_count)
    blocks, replicas, members = groups
    half_index = lax.axis_index("dp") % 2
    half_scalar = half_index.astype(jnp.int32).reshape(1)
    width_part = w_qkv.shape[0]
    local_width = w_qkv.shape[2]
    heads_local, head_part = qkv_bias.shape[1:]
    head_width = head_part * dp_count
    ff_part = shared_down.shape[1]
    expert_part = expert_down.shape[1]

    with scope("ag_qkv"):
        qkv_full = lax.all_gather(
            bf16(w_qkv).reshape(width_part, 3 * local_width), "dp", axis=0, tiled=True
        )
    with scope("ag_bias"):
        bias_full = lax.all_gather(bf16(qkv_bias), "dp", axis=2, tiled=True)
    with scope("ag_in"):
        block_in = gather_over_tensor(inputs)
    with scope("ag_out"):
        out_full = lax.all_gather(bf16(w_out), "dp", axis=0, tiled=True)
    with scope("w_up"):
        expert_up = gather_expert(
            bf16(expert_gate_up).reshape(EXPERTS, 2 * expert_part, width_part), 2, groups
        )
    with scope("w_down"):
        expert_low = gather_expert(bf16(expert_down), 1, groups)
    with scope("ag_cot"):
        grad_rows = gather_over_tensor(cotangent)
    with scope("ag_up"):
        shared_up_full = lax.all_gather(
            bf16(shared_gate_up).reshape(width_part, 2 * ff_part), "dp", axis=0, tiled=True
        )
    with scope("ag_down"):
        shared_down_full = lax.all_gather(bf16(shared_down), "dp", axis=0, tiled=True)

    with scope("slots"):
        expert_ids = jnp.arange(EXPERTS, dtype=jnp.int32)
        named = jnp.any(routes.T[:, None, :] == expert_ids[None, :, None], 0)
        row_ids = jnp.arange(BLOCK, dtype=jnp.int32)
        before = bf16(row_ids[:, None] < row_ids[None, :])
        rank_in = matmul("et,ts->es", bf16(named), before).astype(jnp.int32)
        share = -(-CAP // (8 * tensor_count)) * 8
        slots = EXPERTS * share
        slot_ids = jnp.arange(share, dtype=jnp.int32) + share * lax.axis_index("tensor")
        owned = named[:, None, :] & (rank_in[:, None, :] == slot_ids[None, :, None])
        pick = bf16(owned).reshape(slots, BLOCK)

    def swap_rows(value):
        return swap_groups(bf16(value).reshape(EXPERTS, share, model_width), members).reshape(
            slots, model_width
        )

    with scope("c_swap"):
        slot_cot = bf16(matmul("mt,td->md", pick, grad_rows))
        taken_cot = swap_rows(slot_cot)

    with scope("attn_in"):
        cosine, sine = rope_tables(half_index, head_width)
        normed_first, factor_first = normalize(block_in.astype(jnp.float32))
        first_in = bf16(normed_first * gain_attn)
        projected = matmul("td,dh->th", first_in, qkv_full)
        bias_row = bias_full.astype(jnp.float32).reshape(1, 3 * local_width)
        queries, keys, values = rotate_rows(projected, bias_row, cosine, sine)
    with scope("kv_swap"):
        far_keys = from_partner(keys[:HALF], "dp", 0)
        far_values = from_partner(values[:HALF], "dp", 0)
    with scope("attn_fwd"):
        attended, log_totals = attend(
            half_scalar, queries, keys, values, far_keys, far_values, head_width
        )
    with scope("attn_out"):
        attn_part = bf16(matmul("th,dh->td", attended, out_full))
    with scope("rs_attn"):
        attn_local = sum_over_tensor(attn_part)
    with scope("norm"):
        middle = inputs.astype(jnp.float32) + attn_local
        normed_second, factor_second = normalize(middle)
        second_local = bf16(normed_second * gain_ffn)
    with scope("ag_second"):
        second_in = gather_over_tensor(second_local)
    with scope("t_swap"):
        taken = swap_rows(matmul("mt,td->md", pick, second_in))

    gate_rows = bf16(jnp.concatenate([router, shared_gate[None, :]], 0))
    with scope("router"):
        logits = matmul("ed,td->et", gate_rows, second_in)
        router_probs = jax.nn.softmax(logits[:EXPERTS], 0)
        shared_prob = jax.nn.sigmoid(logits[EXPERTS])
        shared_scale = bf16(shared_prob).astype(jnp.float32)
        gate_values = bf16(router_probs)
        slot_gate = jnp.sum(
            jnp.where(owned, gate_values[:, None, :], 0).astype(jnp.float32), -1
        ).reshape(slots, 1)

    with scope("expert_fwd"):
        pre_act = matmul("cd,fd->cf", taken, expert_up)
        hidden = silu_up(pre_act)
        result = matmul("cf,fd->cd", hidden, expert_low)
    with scope("r_swap"):
        result_back = swap_rows(result)
    with scope("expert_bwd"):
        expert_id = (lax.axis_index("dp") // replicas) * tensor_count + lax.axis_index("tensor")
        taken_probs = jax.nn.softmax(matmul("cd,ed->ce", taken, gate_rows[:EXPERTS]), 1)
        taken_gate = jnp.sum(
            jnp.where(expert_ids[None, :] == expert_id, taken_probs, 0.0), 1, keepdims=True
        )
        taken_gate = bf16(taken_gate).astype(jnp.float32)
        result_grad = bf16(taken_gate * taken_cot.astype(jnp.float32))
        hidden_grad = matmul("cd,fd->cf", result_grad, expert_low)
        pre_grad = bf16(silu_back(pre_act, hidden_grad))
        rows_grad = matmul("cf,fd->cd", pre_grad, expert_up)
    with scope("b_swap"):
        rows_back = swap_rows(rows_grad)

    with scope("shared_fwd"):
        shared_pre = matmul("td,df->tf", second_in, shared_up_full)
        shared_hidden = silu_up(shared_pre)
        shared_result = matmul("tf,df->td", shared_hidden, shared_down_full)
    with scope("shared_bwd"):
        grad_rows_f = grad_rows.astype(jnp.float32)
        shared_scale_grad = jnp.sum(grad_rows_f * shared_result, -1)
        shared_logit_grad = shared_scale_grad * shared_prob * (1.0 - shared_prob)
        shared_result_grad = bf16(shared_scale[:, None] * grad_rows_f)
        shared_hidden_grad = matmul("td,df->tf", shared_result_grad, shared_down_full)
        shared_pre_grad = bf16(silu_back(shared_pre, shared_hidden_grad))
        shared_second = matmul("tf,df->td", shared_pre_grad, shared_up_full)
    with scope("shared_wgrad"):
        shared_down_part = bf16(matmul("td,tf->df", shared_result_grad, shared_hidden))
        shared_up_part = bf16(matmul("td,tf->df", second_in, shared_pre_grad))
    with scope("rs_down"):
        shared_down_grad = lax.psum_scatter(
            shared_down_part, "dp", scatter_dimension=0, tiled=True
        ).astype(jnp.float32)
    with scope("rs_up"):
        shared_up_grad = lax.psum_scatter(
            shared_up_part, "dp", scatter_dimension=0, tiled=True
        ).astype(jnp.float32)

    with scope("expert_wgrad"):
        up_part = bf16(matmul("cf,cd->fd", pre_grad, taken))
        down_part = bf16(matmul("cf,cd->fd", hidden, result_grad))
    with scope("g_down"):
        expert_down_grad = return_expert_grads(down_part, 1, groups).astype(jnp.float32)
    with scope("g_up"):
        expert_up_grad = return_expert_grads(up_part, 2, groups).astype(jnp.float32)

    with scope("mix"):
        gated_pick = pick * bf16(slot_gate)
        combined = matmul("mt,md->td", gated_pick, result_back)
        mixed_part = bf16(combined + shared_scale[:, None] * shared_result)
    with scope("rs_mix"):
        mixed_local = sum_over_tensor(mixed_part)
        layer_out = bf16(middle + mixed_local)

    with scope("gate_grad"):
        slot_grad = jnp.sum(slot_cot.astype(jnp.float32) * result_back.astype(jnp.float32), -1)
        prob_grad = jnp.sum(jnp.where(owned, slot_grad.reshape(EXPERTS, share, 1), 0.0), 1)
        logit_grad = router_probs * (
            prob_grad - jnp.sum(router_probs * prob_grad, 0, keepdims=True)
        )
        logit_grads = bf16(jnp.concatenate([logit_grad, shared_logit_grad[None, :]], 0))
        gate_rows_part = matmul("et,td->ed", logit_grads, second_in)
        early_second = shared_second + matmul("et,ed->td", logit_grads, gate_rows)
    with scope("second_grad"):
        grad_second = bf16(matmul("mt,md->td", pick, rows_back) + early_second)
    with scope("rs_second"):
        second_grad = sum_over_tensor(grad_second)
    with scope("norm_bwd"):
        gain_ffn_part = jnp.sum(second_grad * normed_second, 0)
        middle_grad = cotangent.astype(jnp.float32) + norm_back(
            second_grad, normed_second, factor_second, gain_ffn
        )
    with scope("ag_branch"):
        branch_grad = gather_over_tensor(bf16(middle_grad))
    devices = dp_count * tensor_count
    with scope("gate_sum"):
        gate_parts = jnp.concatenate([gate_rows_part, gain_ffn_part[None, :]], 0)
        gate_parts = gate_parts.reshape(EXPERTS + 2, devices, model_width // devices)
        gate_share = sum_over_all(jnp.transpose(gate_parts, (1, 0, 2)), groups)
    with scope("attn_bwd"):
        attended_grad = bf16(matmul("td,dh->th", branch_grad, out_full))
        (
            query_grad, own_key, own_value, other_key, other_value, near_key, near_value,
        ) = attend_back(
            half_scalar, queries, keys, values, far_keys, far_values,
            attended, log_totals, attended_grad, cosine, sine,
        )
    with scope("kv_back"):
        back_key = from_partner(bf16(other_key), "dp", 0)
        back_value = from_partner(bf16(other_value), "dp", 0)
    with scope("w_out_grad"):
        w_out_part = bf16(matmul("td,th->dh", branch_grad, attended))
        w_out_grad = lax.psum_scatter(
            w_out_part, "dp", scatter_dimension=0, tiled=True
        ).astype(jnp.float32)
    with scope("join"):
        qkv_grad, bias_part = join_grads(
            query_grad, own_key, back_key, near_key, own_value, back_value, near_value, cosine, sine
        )
    with scope("w_qkv_grad"):
        w_qkv_part = bf16(matmul("td,th->dh", first_in, qkv_grad))
        w_qkv_grad = lax.psum_scatter(
            w_qkv_part, "dp", scatter_dimension=0, tiled=True
        ).astype(jnp.float32)
    with scope("first_grad"):
        first_part = bf16(matmul("th,dh->td", qkv_grad, qkv_full))
    with scope("rs_first"):
        first_grad = sum_over_tensor(first_part)
    with scope("last_sum"):
        normed_again = block_in.astype(jnp.float32) * factor_first
        gain_part = jnp.sum(first_part.astype(jnp.float32) * normed_again, 0)
        gain_part = gain_part.reshape(devices, model_width // devices)
        bias_parts = bias_part.reshape(3 * heads_local, dp_count, head_part)
        bias_parts = jnp.transpose(bias_parts, (1, 0, 2)).reshape(dp_count, 1, -1)
        mine = jnp.arange(tensor_count, dtype=jnp.int32) == lax.axis_index("tensor")
        bias_parts = jnp.where(mine[None, :, None], bias_parts, 0.0).reshape(devices, -1)
        last_share = sum_over_all(
            jnp.concatenate([gain_part, bias_parts], 1), groups
        )
        gain_attn_share = last_share[: model_width // devices]
        bias_share = last_share[model_width // devices :].reshape(3, heads_local, head_part)
    with scope("last"):
        local_in = inputs.astype(jnp.float32)
        factor_local = lax.dynamic_slice_in_dim(factor_first, row_start, tok_rows, 0)
        input_grad = middle_grad + norm_back(
            first_grad, local_in * factor_local, factor_local, gain_attn
        )
    return (
        layer_out,
        input_grad,
        gain_attn_share,
        w_qkv_grad.reshape(width_part, 3, local_width),
        bias_share,
        w_out_grad,
        gate_share[EXPERTS + 1],
        gate_share[:EXPERTS],
        gate_share[EXPERTS],
        expert_up_grad.reshape(EXPERTS, 2, expert_part, width_part),
        expert_down_grad,
        shared_up_grad.reshape(width_part, 2, ff_part),
        shared_down_grad,
    )


def solution(mesh):
    return jax.shard_map(
        local,
        mesh=mesh,
        in_specs=(
            P(("dp", "tensor"), None),
            P(("dp", "tensor"), None),
            P("dp", None),
            P(),
            P("dp", None, "tensor"),
            P(None, "tensor", "dp"),
            P("dp", "tensor"),
            P(),
            P(),
            P(),
            P(None, None, "tensor", "dp"),
            P(None, "tensor", "dp"),
            P("dp", None, "tensor"),
            P("dp", "tensor"),
        ),
        out_specs=(
            P(("dp", "tensor"), None),
            P(("dp", "tensor"), None),
            P(("dp", "tensor")),
            P("dp", None, "tensor"),
            P(None, "tensor", "dp"),
            P("dp", "tensor"),
            P(("dp", "tensor")),
            P(None, ("dp", "tensor")),
            P(("dp", "tensor")),
            P(None, None, "tensor", "dp"),
            P(None, "tensor", "dp"),
            P("dp", None, "tensor"),
            P("dp", "tensor"),
        ),
        check_vma=False,
    )
```
